32 devices in a mesh: layer: 2 (over core), row: 4 (over y, x), col: 4 (over z).
Axes of the slice: x: 2, y: 2, z: 4, core: 2. Of those that a mesh axis runs over, the one named last changes fastest.
Arguments:
- amplitudes: float32 [192, 18432], P('row', ('layer', 'col')), may hold values from -6 to 6
- integrals: float32 [18432, 18432], P(('layer', 'col'), 'row'), may hold values from -0.046875 to 0.046875
- other_terms: float32 [192, 18432], P(('layer', 'col'), 'row'), may hold values from -6 to 6
- occupied_sum: float32 [192], P(('layer', 'col')), may hold values from -1.5 to -0.5
- virtual_sum: float32 [18432], P('row'), may hold values from 0.2 to 1.5
Outputs:
- update: float32 [192, 18432], P(('layer', 'col'), 'row')
The draws below stay inside these ranges and needn't reach their ends.
All inputs are finite; a program needn't handle non-finite values.
Results may differ from the reference program's by a relative error of at most 0.00009.
Values sent between devices are 32-bit elements; how exact they have to be, the bound alone decides.
No kernel may reach another device: no remote copies, remote signals or barrier semaphores. Data moves between devices by JAX's collectives and lax.ppermute only.
A program may use at most 128 MiB of HBM per device.

```python
import jax
import jax.numpy as jnp
from jax import lax

K = 18432
N = 18432
M = 192


def raised(array, stream_key, source, target, blocks, factor):
    def block_of(dim):
        return (jnp.arange(array.shape[dim]) // (array.shape[dim] // blocks)).reshape((-1,) + (1,) * (array.ndim - 1 - dim))

    near = jax.random.permutation(stream_key, blocks)[block_of(target)]
    other_side = (block_of(target) + blocks // 2) % blocks
    return jnp.where((block_of(source) == near) | (block_of(source) == other_side), factor * array, array)


def levels(rng, dims, split, low, high):
    def one(dim, blocks):
        steps = jax.random.uniform(jax.random.fold_in(jax.random.fold_in(rng, 6), dim), (blocks,), jnp.float32, low / len(split), high / len(split))
        return jnp.repeat(jnp.exp(steps), dims[dim] // blocks).reshape((-1,) + (1,) * (len(dims) - dim - 1))

    level = one(*split[0])
    for cut in split[1:]:
        level = level * one(*cut)
    return level


def centred(rng, extent, scale, most, pieces=(), kind=jnp.bfloat16):
    gain = levels(rng, extent, pieces, -0.22, 0.18) if pieces else 1.0
    drawn = jax.random.normal(rng, extent, jnp.float32) * scale * gain
    return jnp.minimum(jnp.maximum(drawn, -most), most).astype(kind)


def noise_with(rng, shape, deviation, reach, split, heavy, kind=jnp.bfloat16):
    entries = deviation * jax.random.normal(rng, shape, jnp.float32)
    if split:
        entries = entries * levels(rng, shape, split, -0.22, 0.18)
    return jnp.clip(raised(entries, jax.random.fold_in(rng, 3), *heavy), -reach, reach).astype(kind)


def setup_inputs(seed: int = 0) -> dict:
    streams_of = jax.random.split(jax.random.key(seed), 6)
    return {
        "amplitudes": noise_with(streams_of[0], (M, K), 1.0, 6.0, ((0, 4), (1, 8)), (1, 0, 8, 2.0), jnp.float32),
        "integrals": centred(streams_of[1], (K, N), K ** -0.5, 0.046875, ((0, 8), (1, 4)), jnp.float32),
        "other_terms": centred(streams_of[2], (M, N), 1.0, 6.0, ((0, 8), (1, 4)), jnp.float32),
        "occupied_sum": jnp.clip(-1.5 + 1.0 * jax.random.uniform(streams_of[3], (M,), jnp.float32) ** levels(streams_of[3], (M,), ((0, 8),), -0.2, 0.2), -1.5, -0.5),
        "virtual_sum": jnp.clip(0.2 + 1.3 * jax.random.uniform(streams_of[4], (N,), jnp.float32) ** levels(streams_of[4], (N,), ((0, 4),), -0.2, 0.2), 0.2, 1.5),
    }


def reference(amplitudes, integrals, other_terms, occupied_sum, virtual_sum):
    ladder = jnp.dot(amplitudes, integrals, precision=lax.Precision.HIGHEST, preferred_element_type=jnp.float32)
    residual = other_terms + ladder
    denominator = occupied_sum[:, None] - virtual_sum[None, :]
    return residual / denominator
```

```python
import functools

import jax
import jax.numpy as jnp
from jax import lax
from jax.experimental import pallas as pl
from jax.experimental.pallas import tpu as pltpu
from jax.sharding import PartitionSpec as P


F32 = jnp.float32
BF16 = jnp.bfloat16
SCOPED_BYTES = 8 << 20
CHUNKS = 3
LANES = 128


def bits_of(count):
    return [1 << i for i in range(count.bit_length() - 1)]


def whole(count):
    return [pl.BlockSpec(memory_space=pltpu.VMEM)] * count


def params(limit=SCOPED_BYTES):
    return pltpu.CompilerParams(vmem_limit_bytes=limit)


def swap(array, axis, size, bit):
    return lax.ppermute(array, axis, [(i, i ^ bit) for i in range(size)])


def split_kernel(block_ref, parts_ref):
    step = block_ref.shape[0]
    depth = parts_ref.shape[0] // 2
    start = pl.multiple_of(pl.program_id(0) * step, step)
    block = block_ref[...]
    high = block.astype(BF16)
    parts_ref[pl.ds(start, step), :] = high
    parts_ref[pl.ds(depth + start, step), :] = (block - high.astype(F32)).astype(BF16)


def split_integrals(integrals, ahead):
    depth, width = integrals.shape
    step = 64
    return pl.pallas_call(
        split_kernel,
        grid=(depth // step,),
        in_specs=[pl.BlockSpec((step, width), lambda i: (i, 0))],
        out_specs=pl.BlockSpec(memory_space=pltpu.VMEM),
        out_shape=pltpu.VMEM((2 * depth, width), BF16),
        compiler_params=params(SCOPED_BYTES + ahead),
        cost_estimate=pl.CostEstimate(flops=0, bytes_accessed=4 * depth * width, transcendentals=0),
        name="split_integrals",
    )(integrals)


def arrange_kernel(me_row, me_out, order, *refs):
    pieces, out_ref = refs[:-1], refs[-1]
    rows = out_ref.shape[0] // 2
    dest = rows // (1 << len(order))
    per_piece = pieces[0].shape[0] // dest
    for offset, piece in enumerate(pieces):
        for part in range(per_piece):
            code = ((me_row() ^ offset) * per_piece + part) ^ me_out()
            place = 0
            for level, bit in enumerate(order):
                position = bit.bit_length() - 1
                place += (1 - ((code >> position) & 1)) * (1 << (len(order) - 1 - level))
            start = pl.multiple_of(place * dest, dest)
            values = piece[part * dest : (part + 1) * dest, :]
            high = values.astype(BF16)
            out_ref[pl.ds(start, dest), :] = high
            out_ref[pl.ds(rows + start, dest), :] = (values - high.astype(F32)).astype(BF16)


def arrange(pieces, order, columns):
    rows = pieces[0].shape[0] * len(pieces)
    return pl.pallas_call(
        functools.partial(
            arrange_kernel,
            lambda: lax.axis_index("row"),
            lambda: lax.axis_index("layer") * columns + lax.axis_index("col"),
            order,
        ),
        in_specs=whole(len(pieces)),
        out_specs=pl.BlockSpec(memory_space=pltpu.VMEM),
        out_shape=pltpu.VMEM((2 * rows, pieces[0].shape[1]), BF16),
        compiler_params=params(SCOPED_BYTES - 2 * rows * pieces[0].shape[1] * 2),
        name="arrange",
    )(*pieces)


def product_kernel(start, tile, rows_ref, parts_ref, sent_ref, kept_ref):
    depth = rows_ref.shape[1]
    rows = rows_ref.shape[0] // 2
    half = rows // 2
    width = sent_ref.shape[1]
    for at in range(0, width, tile):
        size = min(tile, width - at)
        columns = slice(start + at, start + at + size)
        both = jnp.dot(rows_ref[...], parts_ref[:depth, columns], preferred_element_type=F32)
        low = jnp.dot(rows_ref[:rows, :], parts_ref[depth:, columns], preferred_element_type=F32)
        total = both[:rows] + (both[rows:] + low)
        sent_ref[:, at : at + size] = total[:half]
        kept_ref[:, at : at + size] = total[half:]


def product(rows, parts, start, width):
    half = rows.shape[0] // 4
    shape = jax.ShapeDtypeStruct((half, width), F32)
    return pl.pallas_call(
        functools.partial(product_kernel, start, 2 * LANES),
        in_specs=whole(2),
        out_specs=whole(2),
        out_shape=[shape, shape],
        compiler_params=params(),
        cost_estimate=pl.CostEstimate(
            flops=6 * rows.shape[0] // 2 * rows.shape[1] * width, bytes_accessed=0, transcendentals=0
        ),
        name="product",
    )(rows, parts)


def cuts(width):
    unit = 2 * LANES if width % (2 * LANES) == 0 else LANES
    count = width // unit
    chunks = min(CHUNKS, count)
    edges = [unit * (count * i // chunks) for i in range(chunks + 1)]
    return list(zip(edges[:-1], edges[1:]))


def shards(sizes, amplitudes, integrals, other_terms, occupied_sum, virtual_sum):
    row_count, layer_count, col_count = sizes
    steps = [("layer", layer_count, bit, bit * col_count) for bit in bits_of(layer_count)]
    steps += [("col", col_count, bit, bit) for bit in bits_of(col_count)]
    order = [code for _, _, _, code in steps]

    pieces = [amplitudes] + [swap(amplitudes, "row", row_count, offset) for offset in range(1, row_count)]
    ahead = row_count * amplitudes.size * amplitudes.dtype.itemsize
    parts = split_integrals(integrals, ahead)
    rows = arrange(pieces, order, col_count)

    results = []
    for start, stop in cuts(integrals.shape[1]):
        sent, kept = product(rows, parts, start, stop - start)
        for number, (axis, size, bit, _) in enumerate(steps):
            taken = swap(sent, axis, size, bit)
            if number + 1 < len(steps):
                half = kept.shape[0] // 2
                sent, kept = kept[:half] + taken[:half], kept[half:] + taken[half:]
            else:
                kept = kept + taken
        denominator = occupied_sum[:, None] - virtual_sum[None, start:stop]
        results.append((other_terms[:, start:stop] + kept) / denominator)
    return jnp.concatenate(results, axis=1)


def solution(mesh):
    sizes = tuple(mesh.shape[axis] for axis in ("row", "layer", "col"))
    return jax.shard_map(
        functools.partial(shards, sizes),
        mesh=mesh,
        in_specs=(
            P("row", ("layer", "col")),
            P(("layer", "col"), "row"),
            P(("layer", "col"), "row"),
            P(("layer", "col")),
            P("row"),
        ),
        out_specs=P(("layer", "col"), "row"),
        check_vma=False,
    )
```
